32 devices in a mesh: dp: 8 (over z, x), shard: 4 (over y, core).
Axes of the slice: x: 2, y: 2, z: 4, core: 2. Of those that a mesh axis runs over, the one named last changes fastest.
Arguments:
- block_in: float32 [32, 256, 1024], P(('dp', 'shard')), may hold values from -6 to 6
- segment_ids: int32 [32, 256], P(('dp', 'shard')), may hold values from 0 to 7, never falling along the last dimension, each value on 1 to 96 neighbouring positions
- out_grad: float32 [32, 256, 1024], P(('dp', 'shard')), may hold values from -6 to 6
- attention_params: float32 [1311744], P(('dp', 'shard')), as said below
- attention_first: float32 [1311744], P(('dp', 'shard')), may hold values from -6 to 6
- attention_second: float32 [1311744], P(('dp', 'shard')), may hold values from 0.1 to 100
- mamba_input_params: float32 [3432448], P(('dp', 'shard')), may hold values from -0.1875 to 0.1875
- mamba_input_first: float32 [3432448], P(('dp', 'shard')), may hold values from -6 to 6
- mamba_input_second: float32 [3432448], P(('dp', 'shard')), may hold values from 0.1 to 100
- mamba_output_params: float32 [1583360], P(('dp', 'shard')), as said below
- mamba_output_first: float32 [1583360], P(('dp', 'shard')), may hold values from -6 to 6
- mamba_output_second: float32 [1583360], P(('dp', 'shard')), may hold values from 0.1 to 100
- swiglu_input_params: float32 [4195328], P(('dp', 'shard')), as said below
- swiglu_input_first: float32 [4195328], P(('dp', 'shard')), may hold values from -6 to 6
- swiglu_input_second: float32 [4195328], P(('dp', 'shard')), may hold values from 0.1 to 100
- swiglu_output_params: float32 [2097152], P(('dp', 'shard')), may hold values from -0.125 to 0.125
- swiglu_output_first: float32 [2097152], P(('dp', 'shard')), may hold values from -6 to 6
- swiglu_output_second: float32 [2097152], P(('dp', 'shard')), may hold values from 0.1 to 100
- mamba_heads_params: float32 [3, 24], replicated, as said below
- mamba_heads_first: float32 [3, 24], replicated, may hold values from -6 to 6
- mamba_heads_second: float32 [3, 24], replicated, may hold values from 0.1 to 100
Outputs:
- block_out: float32 [32, 256, 1024], P(('dp', 'shard'))
- input_grad: float32 [32, 256, 1024], P(('dp', 'shard'))
- attention_grad: float32 [1311744], P(('dp', 'shard'))
- attention_next: float32 [1311744], P(('dp', 'shard'))
- attention_first_next: float32 [1311744], P(('dp', 'shard'))
- attention_second_next: float32 [1311744], P(('dp', 'shard'))
- mamba_input_grad: float32 [3432448], P(('dp', 'shard'))
- mamba_input_next: float32 [3432448], P(('dp', 'shard'))
- mamba_input_first_next: float32 [3432448], P(('dp', 'shard'))
- mamba_input_second_next: float32 [3432448], P(('dp', 'shard'))
- mamba_output_grad: float32 [1583360], P(('dp', 'shard'))
- mamba_output_next: float32 [1583360], P(('dp', 'shard'))
- mamba_output_first_next: float32 [1583360], P(('dp', 'shard'))
- mamba_output_second_next: float32 [1583360], P(('dp', 'shard'))
- swiglu_input_grad: float32 [4195328], P(('dp', 'shard'))
- swiglu_input_next: float32 [4195328], P(('dp', 'shard'))
- swiglu_input_first_next: float32 [4195328], P(('dp', 'shard'))
- swiglu_input_second_next: float32 [4195328], P(('dp', 'shard'))
- swiglu_output_grad: float32 [2097152], P(('dp', 'shard'))
- swiglu_output_next: float32 [2097152], P(('dp', 'shard'))
- swiglu_output_first_next: float32 [2097152], P(('dp', 'shard'))
- swiglu_output_second_next: float32 [2097152], P(('dp', 'shard'))
- mamba_heads_grad: float32 [3, 24], replicated
- mamba_heads_next: float32 [3, 24], replicated
- mamba_heads_first_next: float32 [3, 24], replicated
- mamba_heads_second_next: float32 [3, 24], replicated
The draws below stay inside these ranges and needn't reach their ends.
Inputs may be any that keep to these rules, and one draw needn't show every extreme that they name: attention_params holds a gain near one, a query-key-value projection of fan-in scale and an output projection of four times fan-in scale. mamba_output_params holds convolution taps, a bias, a gain near one and a projection of fan-in scale. swiglu_input_params holds a gain near one followed by a projection of fan-in scale. `mamba_heads_params`: step biases are those of step sizes from 0.001 to 0.1; rates from 1 to 16; skip gains from 0.5 to 1.5.
All inputs are finite; a program needn't handle non-finite values.
Results may differ from the reference program's by a relative error of at most 0.007.
The reference program's roundings to bfloat16 on the way count: a program that leaves them out, or rounds other values in their place, can miss the bound.
Values may be sent and summed in bfloat16 or wider, within the bound.
No kernel may reach another device: no remote copies, remote signals or barrier semaphores. Data moves between devices by JAX's collectives and lax.ppermute only.
A program may use at most 256 MiB of HBM per device.

```python
import math
import jax
import jax.numpy as jnp
import numpy as np
from jax import lax

D = 1024
HD = 64
QH = 8
KVH = 2
MH = 24
NS = 128
FFW = 2048
CONV = 4
STEP = 3
SEQ_LEN = 256
SEQS = 32
U_ATTN = 1311744
U_MIN = 3432448
U_REST = 1583360
U_MLPIN = 4195328
U_MLPOUT = 2097152


def draw_attention_params(key, part):
    subkeys = jax.random.split(key, 3)
    gain_vec = jax.random.uniform(subkeys[0], (D,), jnp.float32, 0.5, 1.5)
    proj_in = jax.random.normal(subkeys[1], (D * (QH + 2 * KVH) * HD,), jnp.float32) * D ** (-0.5)
    proj_out = jax.random.normal(subkeys[2], (QH * HD * D,), jnp.float32) * (4.0 * (QH * HD) ** (-0.5))
    return jnp.concatenate([gain_vec, proj_in, proj_out])


def draw_mamba_output_params(key, part):
    subkeys = jax.random.split(key, 4)
    channels = MH * HD + 2 * NS
    taps = jax.random.normal(subkeys[0], (CONV * channels,), jnp.float32) * 0.5
    bias_row = jax.random.normal(subkeys[1], (channels,), jnp.float32) * 0.3
    gain_vec = jax.random.uniform(subkeys[2], (MH * HD,), jnp.float32, 0.5, 1.5)
    proj_out = jax.random.normal(subkeys[3], (MH * HD * D,), jnp.float32) * (MH * HD) ** (-0.5)
    return jnp.concatenate([taps, bias_row, gain_vec, proj_out])


def draw_swiglu_input_params(key, part):
    subkeys = jax.random.split(key, 2)
    gain_vec = jax.random.uniform(subkeys[0], (D,), jnp.float32, 0.5, 1.5)
    proj_in = jax.random.normal(subkeys[1], (D * 2 * FFW,), jnp.float32) * D ** (-0.5)
    return jnp.concatenate([gain_vec, proj_in])


def draw_mamba_heads_params(key, part):
    subkeys = jax.random.split(key, 3)
    step_sizes = jnp.exp(jax.random.uniform(subkeys[0], (MH,), jnp.float32, jnp.log(0.001), jnp.log(0.1)))
    step_bias = jnp.log(jnp.expm1(step_sizes))
    log_rate = jnp.log(jax.random.uniform(subkeys[1], (MH,), jnp.float32, 1.0, 16.0))
    skip_gain = jax.random.uniform(subkeys[2], (MH,), jnp.float32, 0.5, 1.5)
    return jnp.stack([step_bias, log_rate, skip_gain])


def shard_levels(rng, shape, shards, least, largest):
    def one(dim, shards_of):
        steps = jax.random.uniform(jax.random.fold_in(jax.random.fold_in(rng, 6), dim), (shards_of,), jnp.float32, least / len(shards), largest / len(shards))
        return jnp.repeat(jnp.exp(steps), shape[dim] // shards_of).reshape((-1,) + (1,) * (len(shape) - dim - 1))

    factor_of = one(*shards[0])
    for cut in shards[1:]:
        factor_of = factor_of * one(*cut)
    return factor_of


def length_profile(amount, total, reach, skew):
    weights = [(1 << 20) // math.isqrt(rank ** skew) + 1 for rank in range(2, amount + 1)]
    rest, holding = total - reach - (amount - 1), [1] * (amount - 1)
    while rest > 0:
        movable = [i for i in range(amount - 1) if holding[i] < reach]
        mass, remaining = sum([weights[i] for i in movable]), rest
        for i in movable:
            extra = min(reach - holding[i], max(1, remaining * weights[i] // mass), rest)
            holding[i] = holding[i] + extra
            rest = rest - extra
    return np.array([reach] + holding)


def uneven_parts(stream_key, amount, total, most, slope):
    if amount == 2:
        one = jax.random.randint(stream_key, (), max(1, total - most), min(most, total - 1) + 1)
        return jnp.stack([one, total - one])
    sizes = jnp.asarray(length_profile(amount, total, most, slope), jnp.int32)
    pairs = (amount - 1) // 2
    source_of, taker = sizes[1:1 + 2 * pairs:2], sizes[2:2 + 2 * pairs:2]
    margin = jnp.minimum(source_of - 1, most - taker)
    passed = jax.random.randint(jax.random.fold_in(stream_key, 1), (pairs,), 0, 1 << 20) % (margin + 1)
    sizes = sizes.at[1:1 + 2 * pairs:2].set(source_of - passed).at[2:2 + 2 * pairs:2].set(taker + passed)
    return sizes[jax.random.permutation(jax.random.fold_in(stream_key, 2), amount)]


def scatter_about(own_key, shape, spread, most, shards=(), held_as=jnp.bfloat16):
    values = jax.random.normal(own_key, shape, jnp.float32) * spread
    if len(shards) > 0:
        values = shard_levels(own_key, shape, shards, -0.22, 0.18) * values
    return jnp.clip(values, min=-most, max=most).astype(held_as)


def setup_inputs(seed: int = 0) -> dict:
    seeds = jax.random.split(jax.random.key(seed), 22)
    block_in = scatter_about(seeds[0], (SEQS, SEQ_LEN, D), 1.0, 6.0, ((0, 32),), jnp.float32)
    segment_ids = jax.vmap(lambda own: jnp.searchsorted(jnp.cumsum(uneven_parts(own, 8, SEQ_LEN, SEQ_LEN * 3 // 8, 0)), jnp.arange(SEQ_LEN), side="right"))(jax.random.split(seeds[1], SEQS)).reshape((SEQS, SEQ_LEN)).astype(jnp.int32)
    out_grad = scatter_about(seeds[2], (SEQS, SEQ_LEN, D), 1.0, 6.0, ((0, 32),), jnp.float32)
    attention_params = draw_attention_params(jax.random.fold_in(seeds[21], 71), 0)
    attention_first = scatter_about(seeds[4], (U_ATTN,), 1.0, 6.0, ((0, 32),), jnp.float32)
    attention_second = jnp.clip(jnp.exp(math.log(100.0) - 6.9077553 * jax.random.uniform(seeds[5], (U_ATTN,), jnp.float32) ** shard_levels(seeds[5], (U_ATTN,), ((0, 32),), -0.2, 0.2)), 0.1, 100.0)
    mamba_input_params = scatter_about(seeds[6], (U_MIN,), D ** -0.5, 0.1875, ((0, 32),), jnp.float32)
    mamba_input_first = scatter_about(seeds[7], (U_MIN,), 1.0, 6.0, ((0, 32),), jnp.float32)
    mamba_input_second = jnp.clip(jnp.exp(math.log(100.0) - 6.9077553 * jax.random.uniform(seeds[8], (U_MIN,), jnp.float32) ** shard_levels(seeds[8], (U_MIN,), ((0, 32),), -0.2, 0.2)), 0.1, 100.0)
    mamba_output_params = draw_mamba_output_params(jax.random.fold_in(seeds[21], 71), 0)
    mamba_output_first = scatter_about(seeds[10], (U_REST,), 1.0, 6.0, ((0, 32),), jnp.float32)
    mamba_output_second = jnp.clip(jnp.exp(math.log(100.0) - 6.9077553 * jax.random.uniform(seeds[11], (U_REST,), jnp.float32) ** shard_levels(seeds[11], (U_REST,), ((0, 32),), -0.2, 0.2)), 0.1, 100.0)
    swiglu_input_params = draw_swiglu_input_params(jax.random.fold_in(seeds[21], 71), 0)
    swiglu_input_first = scatter_about(seeds[13], (U_MLPIN,), 1.0, 6.0, ((0, 32),), jnp.float32)
    swiglu_input_second = jnp.clip(jnp.exp(math.log(100.0) - 6.9077553 * jax.random.uniform(seeds[14], (U_MLPIN,), jnp.float32) ** shard_levels(seeds[14], (U_MLPIN,), ((0, 32),), -0.2, 0.2)), 0.1, 100.0)
    swiglu_output_params = scatter_about(seeds[15], (U_MLPOUT,), FFW ** -0.5, 0.125, ((0, 32),), jnp.float32)
    swiglu_output_first = scatter_about(seeds[16], (U_MLPOUT,), 1.0, 6.0, ((0, 32),), jnp.float32)
    swiglu_output_second = jnp.clip(jnp.exp(math.log(100.0) - 6.9077553 * jax.random.uniform(seeds[17], (U_MLPOUT,), jnp.float32) ** shard_levels(seeds[17], (U_MLPOUT,), ((0, 32),), -0.2, 0.2)), 0.1, 100.0)
    mamba_heads_params = draw_mamba_heads_params(jax.random.fold_in(seeds[21], 71), 0)
    mamba_heads_first = scatter_about(seeds[19], (3, MH), 1.0, 6.0, (), jnp.float32)
    mamba_heads_second = jnp.clip(jnp.exp(jax.random.uniform(seeds[20], (3, MH), jnp.float32, math.log(0.1), math.log(100.0))), 0.1, 100.0)
    return {"block_in": block_in, "segment_ids": segment_ids, "out_grad": out_grad, "attention_params": attention_params, "attention_first": attention_first, "attention_second": attention_second, "mamba_input_params": mamba_input_params, "mamba_input_first": mamba_input_first, "mamba_input_second": mamba_input_second, "mamba_output_params": mamba_output_params, "mamba_output_first": mamba_output_first, "mamba_output_second": mamba_output_second, "swiglu_input_params": swiglu_input_params, "swiglu_input_first": swiglu_input_first, "swiglu_input_second": swiglu_input_second, "swiglu_output_params": swiglu_output_params, "swiglu_output_first": swiglu_output_first, "swiglu_output_second": swiglu_output_second, "mamba_heads_params": mamba_heads_params, "mamba_heads_first": mamba_heads_first, "mamba_heads_second": mamba_heads_second}


EPS_NORM = 1e-06
BETA_ONE = 0.9
BETA_TWO = 0.95
RATE = 0.005
DECAY = 0.1
EPS_ADAM = 1e-08

def matmul_rows(left, right):
    return jnp.dot(left, right, preferred_element_type=jnp.float32)

def outer_sum(left, right):
    return lax.dot_general(left, right, (((0,), (0,)), ((), ())), preferred_element_type=jnp.float32)

def back_rows(cotangent, right):
    return lax.dot_general(cotangent, right, (((1,), (1,)), ((), ())), preferred_element_type=jnp.float32)

def norm_rows(features, gain_vec):
    return features * lax.rsqrt(lax.optimization_barrier(jnp.mean(features * features, axis=-1, keepdims=True)) + EPS_NORM) * gain_vec

def swiglu_rows(gate_up):
    return jax.nn.silu(gate_up[:, :FFW]) * gate_up[:, FFW:]

def unpack(vectors):
    attention, mamba_input, mamba_output, swiglu_input, swiglu_output = vectors
    qkv_width = (QH + 2 * KVH) * HD
    inner_width = MH * HD
    channels = inner_width + 2 * NS
    gain_one = attention[:D].astype(jnp.float32)
    w_qkv = attention[D:D + D * qkv_width].reshape(D, qkv_width)
    w_attn_out = attention[D + D * qkv_width:].reshape(QH * HD, D)
    w_mamba_in = mamba_input.reshape(D, 2 * inner_width + 2 * NS + MH)
    tap_end = (CONV + 1) * channels
    tap_rows = mamba_output[:tap_end].reshape(CONV + 1, channels).astype(jnp.float32)
    gain_mix = mamba_output[tap_end:tap_end + inner_width].astype(jnp.float32)
    w_mamba_out = mamba_output[tap_end + inner_width:].reshape(inner_width, D)
    gain_two = swiglu_input[:D].astype(jnp.float32)
    w_gate_up = swiglu_input[D:].reshape(D, 2 * FFW)
    w_down = swiglu_output.reshape(FFW, D)
    return (gain_one, w_qkv, w_attn_out, w_mamba_in, tap_rows, gain_mix, w_mamba_out, gain_two, w_gate_up, w_down)

def pack_grads(grads):
    return (jnp.concatenate([grads[0], grads[1].reshape(-1), grads[2].reshape(-1)]), grads[3].reshape(-1), jnp.concatenate([grads[4].reshape(-1), grads[5], grads[6].reshape(-1)]), jnp.concatenate([grads[7], grads[8].reshape(-1)]), grads[9].reshape(-1))

def attention_core(qkv_rows, allowed):
    seq_count, length, _ = qkv_rows.shape
    group_size = QH // KVH
    query_rows = qkv_rows[..., :QH * HD].reshape(seq_count, length, KVH, group_size, HD)
    key_rows = qkv_rows[..., QH * HD:(QH + KVH) * HD].reshape(seq_count, length, KVH, HD)
    value_rows = qkv_rows[..., (QH + KVH) * HD:].reshape(seq_count, length, KVH, HD)
    scores = jnp.einsum('bskgd,btkd->bkgst', query_rows, key_rows, precision=lax.Precision.HIGHEST) * HD ** (-0.5)
    scores = jnp.where(allowed[:, None, None], scores, -1e+30)
    weights_soft = jax.nn.softmax(scores, axis=-1)
    context = jnp.einsum('bkgst,btkd->bskgd', weights_soft, value_rows, precision=lax.Precision.HIGHEST)
    return context.reshape(seq_count, length, QH * HD)

def mamba_core(projected, tap_rows, gain_mix, head_params, segments, allowed):
    seq_count, length, _ = projected.shape
    inner_width = MH * HD
    channels = inner_width + 2 * NS
    gate_z = projected[..., :inner_width]
    conv_in = projected[..., inner_width:inner_width + channels]
    step_raw = projected[..., inner_width + channels:]
    conv_sum = jnp.zeros_like(conv_in) + tap_rows[CONV]
    for offset in range(CONV):
        lag_steps = CONV - 1 - offset
        if lag_steps == 0:
            conv_sum = conv_sum + tap_rows[offset] * conv_in
        else:
            shifted = jnp.pad(conv_in, ((0, 0), (lag_steps, 0), (0, 0)))[:, :length]
            seg_prev = jnp.pad(segments, ((0, 0), (lag_steps, 0)), constant_values=-1)[:, :length]
            same_segment = (seg_prev == segments)[..., None]
            conv_sum = conv_sum + tap_rows[offset] * jnp.where(same_segment, shifted, 0.0)
    activated = jax.nn.silu(conv_sum)
    states_x = activated[..., :inner_width].reshape(seq_count, length, MH, HD)
    input_b = activated[..., inner_width:inner_width + NS]
    output_c = activated[..., inner_width + NS:]
    step_size = jax.nn.softplus(step_raw + head_params[0])
    cumulative = jnp.cumsum(-step_size * jnp.exp(head_params[1]), axis=1)
    log_spans = cumulative[:, :, None, :] - cumulative[:, None, :, :]
    decay_table = jnp.exp(jnp.where(allowed[..., None], log_spans, -jnp.inf))
    intersection = jnp.einsum('btn,bsn->bts', output_c, input_b, precision=lax.Precision.HIGHEST)
    kernel = intersection[..., None] * decay_table
    weighted = states_x * step_size[..., None]
    scanned = jnp.einsum('btsh,bshp->bthp', kernel, weighted, precision=lax.Precision.HIGHEST)
    scanned = scanned + head_params[2][:, None] * states_x
    gated_rows = scanned.reshape(seq_count, length, inner_width) * jax.nn.silu(gate_z)
    return norm_rows(gated_rows, gain_mix)

def block_pass(pieces, head_params, block_rows, segments, cotangent):
    gain_one, w_qkv, w_attn_out, w_mamba_in, tap_rows, gain_mix, w_mamba_out, gain_two, w_gate_up, w_down = pieces
    seq_count, length, model_width = block_rows.shape
    tokens = seq_count * length
    inner_width = MH * HD
    position = jnp.arange(length)
    causal = position[:, None] >= position[None, :]
    allowed = causal[None] & (segments[:, :, None] == segments[:, None, :])
    flat_rows = block_rows.reshape(tokens, model_width)
    normed, norm_one_back = jax.vjp(norm_rows, flat_rows, gain_one)
    normed_low = normed.astype(jnp.bfloat16)
    qkv_rows = matmul_rows(normed_low, w_qkv)
    projected = matmul_rows(normed_low, w_mamba_in)

    def attend(qkv_now):
        return attention_core(qkv_now.reshape(seq_count, length, -1), allowed).reshape(tokens, QH * HD)
    context, attend_back = jax.vjp(attend, qkv_rows)
    context_low = context.astype(jnp.bfloat16)

    def mixing(proj_now, tap_now, gain_now, head_now):
        return mamba_core(proj_now.reshape(seq_count, length, -1), tap_now, gain_now, head_now, segments, allowed).reshape(tokens, inner_width)
    mix_rows, mix_back = jax.vjp(mixing, projected, tap_rows, gain_mix, head_params)
    mix_low = mix_rows.astype(jnp.bfloat16)
    middle = flat_rows + matmul_rows(context_low, w_attn_out) + matmul_rows(mix_low, w_mamba_out)
    normed_two, norm_two_back = jax.vjp(norm_rows, middle, gain_two)
    normed_two_low = normed_two.astype(jnp.bfloat16)
    gate_up = matmul_rows(normed_two_low, w_gate_up)
    hidden, swiglu_back = jax.vjp(swiglu_rows, gate_up)
    hidden_low = hidden.astype(jnp.bfloat16)
    block_out = middle + matmul_rows(hidden_low, w_down)
    out_cot = cotangent.reshape(tokens, model_width)
    out_cot_low = out_cot.astype(jnp.bfloat16)
    grad_down = outer_sum(hidden_low, out_cot_low)
    grad_hidden = back_rows(out_cot_low, w_down)
    grad_gate_up, = swiglu_back(grad_hidden)
    grad_gate_up_low = grad_gate_up.astype(jnp.bfloat16)
    grad_w_gate_up = outer_sum(normed_two_low, grad_gate_up_low)
    grad_normed_two = back_rows(grad_gate_up_low, w_gate_up)
    grad_middle_norm, grad_gain_two = norm_two_back(grad_normed_two)
    grad_middle = out_cot + grad_middle_norm
    grad_middle_low = grad_middle.astype(jnp.bfloat16)
    grad_w_attn_out = outer_sum(context_low, grad_middle_low)
    grad_w_mamba_out = outer_sum(mix_low, grad_middle_low)
    grad_context = back_rows(grad_middle_low, w_attn_out)
    grad_mix = back_rows(grad_middle_low, w_mamba_out)
    grad_qkv, = attend_back(grad_context)
    grad_projected, grad_taps, grad_gain_mix, grad_heads = mix_back(grad_mix)
    grad_qkv_low = grad_qkv.astype(jnp.bfloat16)
    grad_projected_low = grad_projected.astype(jnp.bfloat16)
    grad_w_qkv = outer_sum(normed_low, grad_qkv_low)
    grad_w_mamba_in = outer_sum(normed_low, grad_projected_low)
    grad_normed = back_rows(grad_qkv_low, w_qkv) + back_rows(grad_projected_low, w_mamba_in)
    grad_rows_norm, grad_gain_one = norm_one_back(grad_normed)
    input_grad = grad_middle + grad_rows_norm
    grads = (grad_gain_one, grad_w_qkv, grad_w_attn_out, grad_w_mamba_in, grad_taps, grad_gain_mix, grad_w_mamba_out, grad_gain_two, grad_w_gate_up, grad_down)
    return (block_out.reshape(block_rows.shape), input_grad.reshape(block_rows.shape), grads, grad_heads)

def adamw(weight_now, moment_one, moment_two, gradient):
    first_next = BETA_ONE * moment_one + (1.0 - BETA_ONE) * gradient
    second_next = BETA_TWO * moment_two + (1.0 - BETA_TWO) * gradient * gradient
    corrected_one = first_next / (1.0 - BETA_ONE ** STEP)
    corrected_two = second_next / (1.0 - BETA_TWO ** STEP)
    weight_next = weight_now - RATE * (corrected_one / (jnp.sqrt(corrected_two) + EPS_ADAM) + DECAY * weight_now)
    return (weight_next, first_next, second_next)

def reference(block_in, segment_ids, out_grad, attention_params, attention_first, attention_second, mamba_input_params, mamba_input_first, mamba_input_second, mamba_output_params, mamba_output_first, mamba_output_second, swiglu_input_params, swiglu_input_first, swiglu_input_second, swiglu_output_params, swiglu_output_first, swiglu_output_second, mamba_heads_params, mamba_heads_first, mamba_heads_second):
    weights = (attention_params, mamba_input_params, mamba_output_params, swiglu_input_params, swiglu_output_params)
    firsts = (attention_first, mamba_input_first, mamba_output_first, swiglu_input_first, swiglu_output_first)
    seconds = (attention_second, mamba_input_second, mamba_output_second, swiglu_input_second, swiglu_output_second)
    pieces = unpack(tuple((weight_now.astype(jnp.bfloat16) for weight_now in weights)))
    per_block = math.gcd(SEQS, max(1, 2048 // SEQ_LEN))
    block_count = SEQS // per_block
    split_rows = block_in.reshape(block_count, per_block, SEQ_LEN, D)
    split_segs = segment_ids.reshape(block_count, per_block, SEQ_LEN)
    split_cots = out_grad.reshape(block_count, per_block, SEQ_LEN, D)

    def scan_step(running, block_slice):
        rows_now, segs_now, cots_now = block_slice
        out_rows, row_grad, grads_now, head_now = block_pass(pieces, mamba_heads_params, rows_now, segs_now, cots_now)
        summed = tuple((earlier + addend for earlier, addend in zip(running[0], grads_now)))
        return ((summed, running[1] + head_now), (out_rows, row_grad))
    start = (tuple((jnp.zeros(piece.shape, jnp.float32) for piece in pieces)), jnp.zeros_like(mamba_heads_params))
    totals, outputs = lax.scan(scan_step, start, (split_rows, split_segs, split_cots))
    grads = pack_grads(totals[0])
    head_grad = totals[1]
    block_out = outputs[0].reshape(SEQS, SEQ_LEN, D)
    input_grad = outputs[1].reshape(SEQS, SEQ_LEN, D)
    updated = [adamw(weights[index], firsts[index], seconds[index], grads[index]) for index in range(5)]
    head_updated = adamw(mamba_heads_params, mamba_heads_first, mamba_heads_second, head_grad)
    return (block_out, input_grad, grads[0], updated[0][0], updated[0][1], updated[0][2], grads[1], updated[1][0], updated[1][1], updated[1][2], grads[2], updated[2][0], updated[2][1], updated[2][2], grads[3], updated[3][0], updated[3][1], updated[3][2], grads[4], updated[4][0], updated[4][1], updated[4][2], head_grad, head_updated[0], head_updated[1], head_updated[2])
```

```python
import functools

import jax
import jax.numpy as jnp
from jax import lax
from jax.experimental import pallas as pl
from jax.experimental.pallas import tpu as pltpu
from jax.sharding import PartitionSpec as P

D = 1024
HD = 64
QH = 8
KVH = 2
MH = 24
NS = 128
FFW = 2048
CONV = 4
STEP = 3


EPS_NORM = 1e-06
BETA_ONE = 0.9
BETA_TWO = 0.95
RATE = 0.005
DECAY = 0.1
EPS_ADAM = 1e-08


def matmul_rows(left, right):
    return jnp.dot(left, right, preferred_element_type=jnp.float32)


def outer_sum(left, right):
    return lax.dot_general(
        left, right, (((0,), (0,)), ((), ())), preferred_element_type=jnp.float32
    )


def outer_low(left, right):
    return outer_sum(left, right).astype(jnp.bfloat16)


def back_rows(cotangent, right):
    return lax.dot_general(
        cotangent, right, (((1,), (1,)), ((), ())), preferred_element_type=jnp.float32
    )


def norm_rows(features, gain_vec):
    return (
        features
        * lax.rsqrt(jnp.mean(features * features, axis=-1, keepdims=True) + EPS_NORM)
        * gain_vec
    )


def swiglu_rows(gate_up):
    return jax.nn.silu(gate_up[:, :FFW]) * gate_up[:, FFW:]


def attention_core(qkv_rows, allowed):
    seq_count, length, _ = qkv_rows.shape
    group_size = QH // KVH
    query_rows = qkv_rows[..., : QH * HD].reshape(seq_count, length, KVH, group_size, HD)
    key_rows = qkv_rows[..., QH * HD : (QH + KVH) * HD].reshape(seq_count, length, KVH, HD)
    value_rows = qkv_rows[..., (QH + KVH) * HD :].reshape(seq_count, length, KVH, HD)
    scores = jnp.einsum(
        "bskgd,btkd->bkgst", query_rows, key_rows, precision=lax.Precision.HIGHEST
    ) * HD ** (-0.5)
    scores = jnp.where(allowed[:, None, None], scores, -1e30)
    weights_soft = jax.nn.softmax(scores, axis=-1)
    context = jnp.einsum(
        "bkgst,btkd->bskgd", weights_soft, value_rows, precision=lax.Precision.HIGHEST
    )
    return context.reshape(seq_count, length, QH * HD)


def mamba_core(projected, tap_rows, gain_mix, head_params, segments, allowed):
    seq_count, length, _ = projected.shape
    inner_width = MH * HD
    channels = inner_width + 2 * NS
    gate_z = projected[..., :inner_width]
    conv_in = projected[..., inner_width : inner_width + channels]
    step_raw = projected[..., inner_width + channels :]
    conv_sum = jnp.zeros_like(conv_in) + tap_rows[CONV]
    for offset in range(CONV):
        lag_steps = CONV - 1 - offset
        if lag_steps == 0:
            conv_sum = conv_sum + tap_rows[offset] * conv_in
        else:
            shifted = jnp.pad(conv_in, ((0, 0), (lag_steps, 0), (0, 0)))[:, :length]
            seg_prev = jnp.pad(segments, ((0, 0), (lag_steps, 0)), constant_values=-1)[:, :length]
            same_segment = (seg_prev == segments)[..., None]
            conv_sum = conv_sum + tap_rows[offset] * jnp.where(same_segment, shifted, 0.0)
    activated = jax.nn.silu(conv_sum)
    states_x = activated[..., :inner_width].reshape(seq_count, length, MH, HD)
    input_b = activated[..., inner_width : inner_width + NS]
    output_c = activated[..., inner_width + NS :]
    step_size = jax.nn.softplus(step_raw + head_params[0])
    cumulative = jnp.cumsum(-step_size * jnp.exp(head_params[1]), axis=1)
    log_spans = cumulative[:, :, None, :] - cumulative[:, None, :, :]
    decay_table = jnp.exp(jnp.where(allowed[..., None], log_spans, -jnp.inf))
    intersection = jnp.einsum("btn,bsn->bts", output_c, input_b, precision=lax.Precision.HIGHEST)
    kernel = intersection[..., None] * decay_table
    weighted = states_x * step_size[..., None]
    scanned = jnp.einsum("btsh,bshp->bthp", kernel, weighted, precision=lax.Precision.HIGHEST)
    scanned = scanned + head_params[2][:, None] * states_x
    gated_rows = scanned.reshape(seq_count, length, inner_width) * jax.nn.silu(gate_z)
    return norm_rows(gated_rows, gain_mix)


def block_pass(pieces, head_params, block_rows, segments, cotangent):
    (
        gain_one,
        w_qkv,
        w_attn_out,
        w_mamba_in,
        tap_rows,
        gain_mix,
        w_mamba_out,
        gain_two,
        w_gate_up,
        w_down,
    ) = pieces
    seq_count, length, model_width = block_rows.shape
    tokens = seq_count * length
    inner_width = MH * HD
    position = jnp.arange(length)
    causal = position[:, None] >= position[None, :]
    allowed = causal[None] & (segments[:, :, None] == segments[:, None, :])
    flat_rows = block_rows.reshape(tokens, model_width)
    normed, norm_one_back = jax.vjp(norm_rows, flat_rows, gain_one)
    normed_low = normed.astype(jnp.bfloat16)
    qkv_rows = matmul_rows(normed_low, w_qkv)
    projected = matmul_rows(normed_low, w_mamba_in)

    def attend(qkv_now):
        return attention_core(qkv_now.reshape(seq_count, length, -1), allowed).reshape(
            tokens, QH * HD
        )

    context, attend_back = jax.vjp(attend, qkv_rows)
    context_low = context.astype(jnp.bfloat16)

    def mixing(proj_now, tap_now, gain_now, head_now):
        return mamba_core(
            proj_now.reshape(seq_count, length, -1), tap_now, gain_now, head_now, segments, allowed
        ).reshape(tokens, inner_width)

    mix_rows, mix_back = jax.vjp(mixing, projected, tap_rows, gain_mix, head_params)
    mix_low = mix_rows.astype(jnp.bfloat16)
    middle = flat_rows + matmul_rows(context_low, w_attn_out) + matmul_rows(mix_low, w_mamba_out)
    normed_two, norm_two_back = jax.vjp(norm_rows, middle, gain_two)
    normed_two_low = normed_two.astype(jnp.bfloat16)
    gate_up = matmul_rows(normed_two_low, w_gate_up)
    hidden, swiglu_back = jax.vjp(swiglu_rows, gate_up)
    hidden_low = hidden.astype(jnp.bfloat16)
    block_out = middle + matmul_rows(hidden_low, w_down)
    out_cot = cotangent.reshape(tokens, model_width)
    out_cot_low = out_cot.astype(jnp.bfloat16)
    grad_down = outer_low(hidden_low, out_cot_low)
    grad_hidden = back_rows(out_cot_low, w_down)
    (grad_gate_up,) = swiglu_back(grad_hidden)
    grad_gate_up_low = grad_gate_up.astype(jnp.bfloat16)
    grad_w_gate_up = outer_low(normed_two_low, grad_gate_up_low)
    grad_normed_two = back_rows(grad_gate_up_low, w_gate_up)
    grad_middle_norm, grad_gain_two = norm_two_back(grad_normed_two)
    grad_middle = out_cot + grad_middle_norm
    grad_middle_low = grad_middle.astype(jnp.bfloat16)
    grad_w_attn_out = outer_low(context_low, grad_middle_low)
    grad_w_mamba_out = outer_low(mix_low, grad_middle_low)
    grad_context = back_rows(grad_middle_low, w_attn_out)
    grad_mix = back_rows(grad_middle_low, w_mamba_out)
    (grad_qkv,) = attend_back(grad_context)
    grad_projected, grad_taps, grad_gain_mix, grad_heads = mix_back(grad_mix)
    grad_qkv_low = grad_qkv.astype(jnp.bfloat16)
    grad_projected_low = grad_projected.astype(jnp.bfloat16)
    grad_w_qkv = outer_low(normed_low, grad_qkv_low)
    grad_w_mamba_in = outer_low(normed_low, grad_projected_low)
    grad_normed = back_rows(grad_qkv_low, w_qkv) + back_rows(grad_projected_low, w_mamba_in)
    grad_rows_norm, grad_gain_one = norm_one_back(grad_normed)
    input_grad = grad_middle + grad_rows_norm
    grads = (
        grad_gain_one,
        grad_w_qkv,
        grad_w_attn_out,
        grad_w_mamba_in,
        grad_taps,
        grad_gain_mix,
        grad_w_mamba_out,
        grad_gain_two,
        grad_w_gate_up,
        grad_down,
    )
    return (
        block_out.reshape(block_rows.shape),
        input_grad.reshape(block_rows.shape),
        grads,
        grad_heads,
    )


def adamw(weight_now, moment_one, moment_two, gradient):
    first_next = BETA_ONE * moment_one + (1.0 - BETA_ONE) * gradient
    second_next = BETA_TWO * moment_two + (1.0 - BETA_TWO) * gradient * gradient
    corrected_one = first_next / (1.0 - BETA_ONE**STEP)
    corrected_two = second_next / (1.0 - BETA_TWO**STEP)
    weight_next = weight_now - RATE * (
        corrected_one / (jnp.sqrt(corrected_two) + EPS_ADAM) + DECAY * weight_now
    )
    return (weight_next, first_next, second_next)


AXES = ("dp", "shard")


def swap(values, count, bit):
    return lax.ppermute(values, AXES, [(i, i ^ (1 << bit)) for i in range(count)])


def stage_orders(bits, rows):
    rest = list(range(3, bits))
    if bits < 3 or rows % 32:
        return [list(range(1, bits))]
    return [[2, 1] + rest, [1, 2] + rest]


def assemble(index, halves, partners, orders, bits, rows, width):
    pairs = 1 << (bits - 1)
    part = rows // len(orders)

    def place_for(order):
        gathered = order[::-1]

        def place(step, where):
            relative = step ^ (where[0] >> 1)
            slot = 0
            for position, bit in enumerate(gathered):
                slot = slot | (((relative >> (bit - 1)) & 1) << position)
            return (slot, 0, 0)

        return place

    def body(where, *refs):
        out = refs[-1]
        odd = where[0] & 1
        for color in range(len(orders)):
            span = pl.ds(color * part, part)
            own, other = refs[2 * color], refs[2 * color + 1]

            @pl.when(odd == 0)
            def _():
                out[0, 0, span, :] = own[0]
                out[0, 1, span, :] = other[0]

            @pl.when(odd == 1)
            def _():
                out[0, 1, span, :] = own[0]
                out[0, 0, span, :] = other[0]

    operands, specs = [], []
    for order, own, other in zip(orders, halves, partners):
        for piece in (own, other):
            operands.append(piece)
            specs.append(pl.BlockSpec((1, part, width), place_for(order)))
    whole = pl.pallas_call(
        body,
        out_shape=jax.ShapeDtypeStruct((pairs, 2, rows, width), jnp.bfloat16),
        grid_spec=pltpu.PrefetchScalarGridSpec(
            num_scalar_prefetch=1,
            grid=(pairs,),
            in_specs=specs,
            out_specs=pl.BlockSpec((1, 2, rows, width), lambda step, where: (step, 0, 0, 0)),
        ),
        cost_estimate=pl.CostEstimate(
            flops=0, transcendentals=0, bytes_accessed=8 * pairs * rows * width
        ),
        name="assemble",
    )(index, *operands)
    return whole.reshape(2 * pairs * rows, width)


def gather_rows(block, index, count):
    rows, width = block.shape
    bits = count.bit_length() - 1
    orders = stage_orders(bits, rows)
    part = rows // len(orders)
    halves, partners = [], []
    for color, order in enumerate(orders):
        held = block[color * part : (color + 1) * part][None]
        for bit in order[::-1]:
            held = jnp.concatenate([held, swap(held, count, bit)], axis=0)
        halves.append(held)
        partners.append(swap(held, count, 0))
    return assemble(index, halves, partners, orders, bits, rows, width)


def take(term, mine, done, bit, span):
    array, left, first = term
    lead = array.ndim - 2
    starts, sizes = [], []
    for own in left:
        if own == bit:
            starts.append(1 - mine[own])
            sizes.append(1)
        elif own in done:
            starts.append(mine[own])
            sizes.append(1)
        else:
            starts.append(0)
            sizes.append(2)
    starts += [span[0] - first, 0]
    sizes += [span[1] - span[0], array.shape[-1]]
    piece = lax.dynamic_slice(array, starts, sizes)
    return piece.reshape([2] * sum(size == 2 for size in sizes[:lead]) + sizes[lead:])


def total(terms, mine, done, bit, span):
    out = None
    for term in terms:
        piece = take(term, mine, done, bit, span).astype(jnp.float32)
        out = piece if out is None else out + piece
    return out


def scatter_rows(values, mine, count):
    bits = count.bit_length() - 1
    rows, width = values.shape[0] // count, values.shape[1]
    falling = list(range(bits))[::-1]
    first = (values.reshape([2] * bits + [rows, width]), falling, 0)
    sent = total([first], mine, [], 0, (0, rows)).astype(jnp.bfloat16)
    second = (swap(sent, count, 0), falling[:-1], 0)
    orders = stage_orders(bits, rows)
    part = rows // len(orders)
    pieces = []
    for color, order in enumerate(orders):
        span = (color * part, (color + 1) * part)
        terms, done = [first, second], [0]
        left = falling[:-1]
        for bit in order:
            sent = total(terms, mine, done, bit, span).astype(jnp.bfloat16)
            left = [own for own in left if own != bit]
            terms.append((swap(sent, count, bit), left, span[0]))
            done = done + [bit]
        pieces.append(total(terms, mine, done, None, span))
    return jnp.concatenate(pieces, axis=0) if len(pieces) > 1 else pieces[0]


def local(
    dp_size,
    shard_size,
    block_in,
    segment_ids,
    out_grad,
    attention_params,
    attention_first,
    attention_second,
    mamba_input_params,
    mamba_input_first,
    mamba_input_second,
    mamba_output_params,
    mamba_output_first,
    mamba_output_second,
    swiglu_input_params,
    swiglu_input_first,
    swiglu_input_second,
    swiglu_output_params,
    swiglu_output_first,
    swiglu_output_second,
    mamba_heads_params,
    mamba_heads_first,
    mamba_heads_second,
):
    count = dp_size * shard_size
    bits = count.bit_length() - 1
    device = lax.axis_index("dp") * shard_size + lax.axis_index("shard")
    mine = [(device >> bit) & 1 for bit in range(bits)]
    index = device.astype(jnp.int32).reshape(1)
    qkv_width = (QH + 2 * KVH) * HD
    inner_width = MH * HD
    channels = inner_width + 2 * NS
    tap_end = (CONV + 1) * channels
    head_sizes = (D, tap_end + inner_width, D)
    packed = (attention_params, mamba_output_params, swiglu_input_params)
    widths = (128, D, 2 * FFW)
    heads = jnp.concatenate(
        [vector[:size] for vector, size in zip(packed, head_sizes)]
    ).astype(jnp.bfloat16)
    lent = lax.ppermute(heads, AXES, [(i + 1, i) for i in range(count - 1)])
    whole_heads = lax.psum(
        jnp.where(device == 0, heads.astype(jnp.float32), 0.0), AXES
    )
    cuts = (0, head_sizes[0], head_sizes[0] + head_sizes[1], sum(head_sizes))
    blocks = []
    for position, (vector, size, width) in enumerate(zip(packed, head_sizes, widths)):
        share = size // count
        joined = jnp.concatenate(
            [vector.astype(jnp.bfloat16), lent[cuts[position] : cuts[position + 1]]]
        )
        aligned = lax.dynamic_slice(
            joined, (share * (count - device),), (vector.shape[0] - share,)
        )
        blocks.append(aligned.reshape(-1, width))
    proj_width = 2 * inner_width + 2 * NS + MH
    in_block = mamba_input_params.astype(jnp.bfloat16).reshape(-1, proj_width)
    down_block = swiglu_output_params.astype(jnp.bfloat16).reshape(-1, D)
    attn_whole = gather_rows(blocks[0], index, count)
    w_mamba_in = gather_rows(in_block, index, count)
    w_mamba_out = gather_rows(blocks[1], index, count)
    w_gate_up = gather_rows(blocks[2], index, count)
    w_down = gather_rows(down_block, index, count)
    qkv_lines = D * qkv_width // 128
    w_qkv = attn_whole[:qkv_lines].reshape(D, qkv_width)
    w_attn_out = attn_whole[qkv_lines:].reshape(QH * HD, D)
    gain_one = whole_heads[: cuts[1]]
    tap_rows = whole_heads[cuts[1] : cuts[1] + tap_end].reshape(CONV + 1, channels)
    gain_mix = whole_heads[cuts[1] + tap_end : cuts[2]]
    gain_two = whole_heads[cuts[2] :]
    pieces = (
        gain_one,
        w_qkv,
        w_attn_out,
        w_mamba_in,
        tap_rows,
        gain_mix,
        w_mamba_out,
        gain_two,
        w_gate_up,
        w_down,
    )
    block_out, input_grad, grads, head_local = block_pass(
        pieces, mamba_heads_params, block_in, segment_ids, out_grad
    )
    down_rows = scatter_rows(grads[9], mine, count)
    gate_rows = scatter_rows(grads[8], mine, count)
    mix_rows = scatter_rows(grads[6], mine, count)
    attn_lines = jnp.concatenate([grads[1].reshape(-1, 128), grads[2].reshape(-1, 128)])
    attn_rows = scatter_rows(attn_lines, mine, count)
    in_rows = scatter_rows(grads[3], mine, count)
    small = jnp.concatenate(
        [grads[0], grads[4].reshape(-1), grads[5], grads[7], head_local.reshape(-1)]
    )
    small = lax.psum(small, AXES)
    head_grad = small[cuts[3] :].reshape(head_local.shape)
    packed_grads = []
    for position, (rows_now, size) in enumerate(
        zip((attn_rows, mix_rows, gate_rows), head_sizes)
    ):
        share = size // count
        flat = rows_now.reshape(-1)
        ahead = lax.ppermute(
            flat[flat.shape[0] - size :], AXES, [(i, i + 1) for i in range(count - 1)]
        )
        ahead = jnp.where(device == 0, small[cuts[position] : cuts[position + 1]], ahead)
        joined = jnp.concatenate([ahead, flat])
        packed_grads.append(
            lax.dynamic_slice(joined, (share * device,), (flat.shape[0] + share,))
        )
    reduced = (
        packed_grads[0],
        in_rows.reshape(-1),
        packed_grads[1],
        packed_grads[2],
        down_rows.reshape(-1),
    )
    owned = (
        attention_params,
        mamba_input_params,
        mamba_output_params,
        swiglu_input_params,
        swiglu_output_params,
    )
    firsts = (
        attention_first,
        mamba_input_first,
        mamba_output_first,
        swiglu_input_first,
        swiglu_output_first,
    )
    seconds = (
        attention_second,
        mamba_input_second,
        mamba_output_second,
        swiglu_input_second,
        swiglu_output_second,
    )
    outputs = [block_out, input_grad]
    for gradient, weight_now, first, second in zip(reduced, owned, firsts, seconds):
        outputs.append(gradient)
        outputs.extend(adamw(weight_now, first, second, gradient))
    outputs.append(head_grad)
    outputs.extend(
        adamw(mamba_heads_params, mamba_heads_first, mamba_heads_second, head_grad)
    )
    return tuple(outputs)


def solution(mesh):
    in_specs = (
        P(("dp", "shard"), None, None),
        P(("dp", "shard"), None),
        P(("dp", "shard"), None, None),
        P(("dp", "shard")),
        P(("dp", "shard")),
        P(("dp", "shard")),
        P(("dp", "shard")),
        P(("dp", "shard")),
        P(("dp", "shard")),
        P(("dp", "shard")),
        P(("dp", "shard")),
        P(("dp", "shard")),
        P(("dp", "shard")),
        P(("dp", "shard")),
        P(("dp", "shard")),
        P(("dp", "shard")),
        P(("dp", "shard")),
        P(("dp", "shard")),
        P(),
        P(),
        P(),
    )
    out_specs = (
        P(("dp", "shard"), None, None),
        P(("dp", "shard"), None, None),
        P(("dp", "shard")),
        P(("dp", "shard")),
        P(("dp", "shard")),
        P(("dp", "shard")),
        P(("dp", "shard")),
        P(("dp", "shard")),
        P(("dp", "shard")),
        P(("dp", "shard")),
        P(("dp", "shard")),
        P(("dp", "shard")),
        P(("dp", "shard")),
        P(("dp", "shard")),
        P(("dp", "shard")),
        P(("dp", "shard")),
        P(("dp", "shard")),
        P(("dp", "shard")),
        P(("dp", "shard")),
        P(("dp", "shard")),
        P(("dp", "shard")),
        P(("dp", "shard")),
        P(),
        P(),
        P(),
        P(),
    )
    step = functools.partial(local, mesh.shape["dp"], mesh.shape["shard"])
    return jax.shard_map(step, mesh=mesh, in_specs=in_specs, out_specs=out_specs, check_vma=False)
```
